512 devices in a mesh: space: 32 (over y, z_lo), mode: 16 (over z_hi, x, core).
Axes of the slice: x: 4, y: 8, z: 8 (z_hi: 2, z_lo: 4; z = z_hi * 4 + z_lo), core: 2. Of those that a mesh axis runs over, the one named last changes fastest.
Arguments:
- left_modes: bfloat16 [2, 12, 4096, 4096], P(None, None, 'space', 'mode'), may hold values from -6 to 6
- right_modes: bfloat16 [32, 2, 12, 4096], P('mode', None, None, 'space'), may hold values from -6 to 6
- momenta: int32 [16, 3], replicated, may hold values from -2 to 2
- coords: int32 [3, 4096], P(None, 'space'), may hold values from 0 to 95
Outputs:
- meson_field: float32 [4096, 16, 2, 32], P(('mode', 'space'))
The draws below stay inside these ranges and needn't reach their ends.
All inputs are finite; a program needn't handle non-finite values.
Results may differ from the reference program's by a relative error of at most 0.0028.
Values may be sent and summed in bfloat16 or wider, within the bound.
No kernel may reach another device: no remote copies, remote signals or barrier semaphores. Data moves between devices by JAX's collectives and lax.ppermute only.
A program may use at most 64 MiB of HBM per device.

```python
import math
import jax
import jax.numpy as jnp
from jax import lax

EXTENT = 96
P_SIZE = 16
LEFT = 4096
R_DEV = 2
RIGHT = 32
SITES = 4096


def touch_ends(entries, stream_key, smallest, high):
    shape = entries.shape
    place = [jax.random.randint(jax.random.fold_in(stream_key, axis), (), 0, shape[axis]) for axis in range(len(shape))]
    entries = entries.at[tuple(place)].set(smallest)
    longest = shape.index(max(shape))
    place[longest] = (place[longest] + 1) % shape[longest]
    return entries.at[tuple(place)].set(high)


def shard_levels(own_key, dims, shards, low, top_value):
    def one(position, parts):
        steps = jax.random.uniform(jax.random.fold_in(jax.random.fold_in(own_key, 6), position), (parts,), jnp.float32, low / len(shards), top_value / len(shards))
        return jnp.repeat(jnp.exp(steps), dims[position] // parts).reshape((-1,) + (1,) * (len(dims) - position - 1))

    level = one(*shards[0])
    for cut in shards[1:]:
        level = level * one(*cut)
    return level


def normal_values(rng, shape, deviation, most, cuts=(), kind=jnp.bfloat16):
    drawn = jax.random.normal(rng, shape, jnp.float32) * deviation
    if len(cuts) > 0:
        drawn = shard_levels(rng, shape, cuts, -0.22, 0.18) * drawn
    return jnp.clip(drawn, min=-most, max=most).astype(kind)


def setup_inputs(seed: int = 0) -> dict:
    key_of = jax.random.split(jax.random.key(seed), 5)
    left_modes = normal_values(key_of[0], (2, 12, SITES, LEFT), 1.0, 6.0, ((2, 32), (3, 16)))
    right_modes = normal_values(key_of[1], (RIGHT, 2, 12, SITES), 1.0, 6.0, ((0, 16), (3, 32)))
    momenta = touch_ends(jax.random.randint(key_of[2], (P_SIZE, 3), -2, 3), jax.random.fold_in(key_of[2], 1), -2, 2).astype(jnp.int32)
    coords = touch_ends(jax.random.randint(key_of[3], (3, SITES), 0, EXTENT), jax.random.fold_in(key_of[3], 1), 0, EXTENT - 1).astype(jnp.int32)
    return {"left_modes": left_modes, "right_modes": right_modes, "momenta": momenta, "coords": coords}


def phase_tables(momenta, coords):
    phase_turns = jnp.mod(lax.optimization_barrier(jnp.sum(momenta[:, :, None] * coords[None, :, :], axis=1)), EXTENT)
    angles = phase_turns.astype(jnp.float32) * (2.0 * math.pi / EXTENT)
    return (jnp.cos(angles), jnp.sin(angles))

def phased_block(right_piece, cosines, sines):
    piece_rows = right_piece.shape[0]
    real_part = right_piece[:, 0].astype(jnp.float32)[None]
    imag_part = right_piece[:, 1].astype(jnp.float32)[None]
    cos_wide = cosines[:, None, None, :]
    sin_wide = sines[:, None, None, :]
    turned_re = (cos_wide * real_part + sin_wide * imag_part).astype(jnp.bfloat16)
    turned_im = (cos_wide * imag_part - sin_wide * real_part).astype(jnp.bfloat16)
    upper_half = jnp.stack([turned_re, turned_im], axis=2)
    lower_half = jnp.stack([turned_im, -turned_re], axis=2)
    stacked = jnp.stack([upper_half, lower_half], axis=1)
    return stacked.reshape(cosines.shape[0] * 2 * piece_rows, -1)

def reference(left_modes, right_modes, momenta, coords):
    cosines, sines = phase_tables(momenta, coords)
    left_mat = left_modes.reshape(-1, LEFT)
    blocks = right_modes.reshape(RIGHT // R_DEV, R_DEV, 2, 12, SITES)

    def one_block(right_piece):
        stacked = phased_block(right_piece, cosines, sines)
        return jnp.dot(stacked, left_mat, preferred_element_type=jnp.float32)
    tiles = lax.map(one_block, blocks)
    tiles = tiles.reshape(RIGHT // R_DEV, P_SIZE, 2, R_DEV, LEFT)
    tiles = jnp.transpose(tiles, (4, 1, 2, 0, 3)).reshape(LEFT, P_SIZE, 2, RIGHT)
    return tiles * (1.0 / math.sqrt(12 * SITES))
```

```python
import functools
import math

import jax
import jax.numpy as jnp
from jax import lax
from jax.experimental import pallas as pl
from jax.experimental.pallas import tpu as pltpu
from jax.sharding import PartitionSpec as P

EXTENT = 96


def phase_tables(momenta, coords):
    phase_turns = jnp.mod(jnp.sum(momenta[:, :, None] * coords[None, :, :], axis=1), EXTENT)
    angles = phase_turns.astype(jnp.float32) * (2.0 * math.pi / EXTENT)
    return (jnp.cos(angles), jnp.sin(angles))


def partial_kernel(left_ref, right_ref, cos_ref, sin_ref, out_ref):
    rows, depth = right_ref.shape
    modes = rows // 2
    comps = depth // cos_ref.shape[1]
    row = lax.broadcasted_iota(jnp.int32, (rows, rows), 0)
    col = lax.broadcasted_iota(jnp.int32, (rows, rows), 1)
    mode, part = row % modes, row // modes
    pick = jnp.where(col == 2 * mode + part, 1.0, 0.0).astype(jnp.bfloat16)
    sign = jnp.where(part == 0, 1.0, -1.0)
    swap = jnp.where(col == 2 * mode + 1 - part, sign, 0.0).astype(jnp.bfloat16)
    plain = jnp.dot(pick, right_ref[...], preferred_element_type=jnp.float32)
    other = jnp.dot(swap, right_ref[...], preferred_element_type=jnp.float32)
    for p in range(cos_ref.shape[0]):
        cos_row = jnp.concatenate([cos_ref[p : p + 1, :]] * comps, axis=1)
        sin_row = jnp.concatenate([sin_ref[p : p + 1, :]] * comps, axis=1)
        first = (cos_row * plain + sin_row * other).astype(jnp.bfloat16)
        second = (cos_row * other - sin_row * plain).astype(jnp.bfloat16)
        tile = jnp.dot(first, left_ref[0], preferred_element_type=jnp.float32)
        tile += jnp.dot(second, left_ref[1], preferred_element_type=jnp.float32)
        out_ref[:, p * rows : (p + 1) * rows] = tile.T.astype(out_ref.dtype)


def partial_tile(left, right, cosines, sines):
    rows, depth = right.shape
    columns = left.shape[2]
    return pl.pallas_call(
        partial_kernel,
        out_shape=jax.ShapeDtypeStruct((columns, cosines.shape[0] * rows), jnp.bfloat16),
        in_specs=[pl.BlockSpec(memory_space=pltpu.VMEM)] * 4,
        out_specs=pl.BlockSpec(memory_space=pltpu.VMEM),
        compiler_params=pltpu.CompilerParams(vmem_limit_bytes=40 << 20),
    )(left, right, cosines, sines)


def body(left_modes, right_modes, momenta, coords):
    cosines, sines = phase_tables(momenta, coords)
    space, mode = lax.axis_size("space"), lax.axis_size("mode")
    held, _, comps, sites = right_modes.shape
    columns = left_modes.shape[-1]
    momentum_count = momenta.shape[0]
    norm_scale = 1.0 / math.sqrt(comps * sites * space)
    own = right_modes.reshape(1, 2 * held, comps * sites)
    right = lax.all_to_all(jnp.broadcast_to(own, (mode,) + own.shape[1:]), "mode", 0, 0, tiled=True)
    right = right.reshape(mode * 2 * held, comps * sites)
    left = left_modes.reshape(2, comps * sites, columns)
    tile = partial_tile(left, right, cosines, sines)
    pieces = tile.reshape(space, columns // space, tile.shape[1])
    owned = lax.all_to_all(pieces, "space", 0, 0, tiled=True)
    summed = jnp.sum(owned.astype(jnp.float32), axis=0) * norm_scale
    return summed.reshape(columns // space, momentum_count, 2, mode * held)


def solution(mesh):
    in_specs = (
        P(None, None, "space", "mode"),
        P("mode", None, None, "space"),
        P(),
        P(None, "space"),
    )
    out_specs = P(("mode", "space"), None, None, None)
    return jax.shard_map(body, mesh=mesh, in_specs=in_specs, out_specs=out_specs, check_vma=False)
```

```python
import math

import jax
import jax.numpy as jnp
from jax import lax
from jax.experimental import pallas as pl
from jax.experimental.pallas import tpu as pltpu
from jax.sharding import PartitionSpec as P

EXTENT = 96
GROUP = 4
NT = (((1,), (1,)), ((), ()))


def phase_tables(momenta, coords):
    phase_turns = jnp.mod(jnp.sum(momenta[:, :, None] * coords[None, :, :], axis=1), EXTENT)
    angles = phase_turns.astype(jnp.float32) * (2.0 * math.pi / EXTENT)
    return (jnp.cos(angles), jnp.sin(angles))


def turn_kernel(left_ref, out_ref):
    columns = left_ref.shape[2]
    for part in range(2):
        out_ref[part * columns : (part + 1) * columns, :] = left_ref[part].T


def turned_left(left):
    _, depth, columns = left.shape
    return pl.pallas_call(
        turn_kernel,
        out_shape=jax.ShapeDtypeStruct((2 * columns, depth), left.dtype),
        in_specs=[pl.BlockSpec(memory_space=pltpu.VMEM)],
        out_specs=pl.BlockSpec(memory_space=pltpu.VMEM),
        cost_estimate=pl.CostEstimate(flops=0, transcendentals=0, bytes_accessed=4 * left.size),
        compiler_params=pltpu.CompilerParams(vmem_limit_bytes=16 << 20),
        name="turn_left",
    )(left)


def partial_kernel(left_ref, right_ref, cos_ref, sin_ref, out_ref, plain_ref, rows_ref):
    momenta, sites = cos_ref.shape
    depth = left_ref.shape[1]
    comps = depth // sites
    modes = right_ref.shape[0] // (2 * comps)
    columns = out_ref.shape[0]
    half = GROUP * modes
    plain_ref[...] = right_ref[...].astype(jnp.float32)
    for q in range(momenta // GROUP):
        slot = q % 2
        for c in range(comps):
            real = plain_ref[pl.ds(2 * c, modes, stride=2 * comps), :]
            imag = plain_ref[pl.ds(2 * c + 1, modes, stride=2 * comps), :]
            lanes = slice(c * sites, (c + 1) * sites)
            for k in range(GROUP):
                p = q * GROUP + k
                cos_row, sin_row = cos_ref[p : p + 1, :], sin_ref[p : p + 1, :]
                turned_re = (cos_row * real + sin_row * imag).astype(jnp.bfloat16)
                turned_im = (cos_row * imag - sin_row * real).astype(jnp.bfloat16)
                rows_ref[slot, k * modes : (k + 1) * modes, lanes] = turned_re
                rows_ref[slot, half + k * modes : half + (k + 1) * modes, lanes] = turned_im
        both = lax.dot_general(left_ref[...], rows_ref[slot], NT, preferred_element_type=jnp.float32)
        upper, lower = both[:columns], both[columns:]
        base = q * 2 * half
        out_ref[:, base : base + half] = (upper[:, :half] + lower[:, half:]).astype(out_ref.dtype)
        out_ref[:, base + half : base + 2 * half] = (upper[:, half:] - lower[:, :half]).astype(out_ref.dtype)


def partial_tile(left, right, cosines, sines):
    rows, sites = right.shape
    columns, depth = left.shape[0] // 2, left.shape[1]
    modes = rows * sites // (2 * depth)
    momenta = cosines.shape[0]
    return pl.pallas_call(
        partial_kernel,
        out_shape=jax.ShapeDtypeStruct((columns, momenta * 2 * modes), jnp.bfloat16),
        in_specs=[pl.BlockSpec(memory_space=pltpu.VMEM)] * 4,
        out_specs=pl.BlockSpec(memory_space=pltpu.VMEM),
        scratch_shapes=[
            pltpu.VMEM((rows, sites), jnp.float32),
            pltpu.VMEM((2, 2 * GROUP * modes, depth), jnp.bfloat16),
        ],
        compiler_params=pltpu.CompilerParams(vmem_limit_bytes=32 << 20),
        name="partial_tile",
    )(left, right, cosines, sines)


def sum_kernel(scale, pieces_ref, out_ref):
    _, momenta, parts, modes = out_ref.shape
    total = jnp.sum(pieces_ref[...].astype(jnp.float32), axis=0) * scale
    for p in range(momenta):
        for part in range(parts):
            group, k = divmod(p, GROUP)
            start = ((group * parts + part) * GROUP + k) * modes
            out_ref[:, p, part, :] = total[:, start : start + modes]


def owned_sum(pieces, momenta, scale):
    _, rows, width = pieces.shape
    return pl.pallas_call(
        lambda a, b: sum_kernel(scale, a, b),
        out_shape=jax.ShapeDtypeStruct((rows, momenta, 2, width // (2 * momenta)), jnp.float32),
        in_specs=[pl.BlockSpec(memory_space=pltpu.VMEM)],
        out_specs=pl.BlockSpec(memory_space=pltpu.VMEM),
        compiler_params=pltpu.CompilerParams(vmem_limit_bytes=8 << 20),
        name="owned_sum",
    )(pieces)


def body(left_modes, right_modes, momenta, coords):
    cosines, sines = phase_tables(momenta, coords)
    space, mode = lax.axis_size("space"), lax.axis_size("mode")
    held, _, comps, sites = right_modes.shape
    columns = left_modes.shape[-1]
    norm_scale = 1.0 / math.sqrt(comps * sites * space)
    own = right_modes.transpose(0, 2, 1, 3).reshape(1, held * comps * 2, sites)
    right = lax.all_to_all(jnp.broadcast_to(own, (mode,) + own.shape[1:]), "mode", 0, 0, tiled=True)
    left = turned_left(left_modes.reshape(2, comps * sites, columns))
    tile = partial_tile(left, right.reshape(-1, sites), cosines, sines)
    pieces = tile.reshape(space, columns // space, tile.shape[1])
    owned = lax.all_to_all(pieces, "space", 0, 0, tiled=True)
    return owned_sum(owned, momenta.shape[0], norm_scale)


def solution(mesh):
    in_specs = (
        P(None, None, "space", "mode"),
        P("mode", None, None, "space"),
        P(),
        P(None, "space"),
    )
    out_specs = P(("mode", "space"), None, None, None)
    return jax.shard_map(body, mesh=mesh, in_specs=in_specs, out_specs=out_specs, check_vma=False)
```

```python
import functools
import math

import jax
import jax.numpy as jnp
from jax import lax
from jax.experimental import pallas as pl
from jax.experimental.pallas import tpu as pltpu
from jax.sharding import PartitionSpec as P

EXTENT = 96
GROUP = 4
MODE_FIRST = 15
SPACE_FIRST = 30
NT = (((1,), (1,)), ((), ()))


def phase_tables(momenta, coords):
    phase_turns = jnp.mod(jnp.sum(momenta[:, :, None] * coords[None, :, :], axis=1), EXTENT)
    angles = phase_turns.astype(jnp.float32) * (2.0 * math.pi / EXTENT)
    return (jnp.cos(angles), jnp.sin(angles))


def led_by(first, count):
    return [(first + k) % count for k in range(count)]


def turn_kernel(skip, left_ref, out_ref):
    columns = left_ref.shape[2]
    for part in range(2):
        turned = left_ref[part].T
        base = part * columns
        out_ref[base : base + columns - skip, :] = turned[skip:, :]
        out_ref[base + columns - skip : base + columns, :] = turned[:skip, :]


def turned_left(left, skip):
    _, depth, columns = left.shape
    return pl.pallas_call(
        functools.partial(turn_kernel, skip),
        out_shape=jax.ShapeDtypeStruct((2 * columns, depth), left.dtype),
        in_specs=[pl.BlockSpec(memory_space=pltpu.VMEM)],
        out_specs=pl.BlockSpec(memory_space=pltpu.VMEM),
        cost_estimate=pl.CostEstimate(flops=0, transcendentals=0, bytes_accessed=4 * left.size),
        compiler_params=pltpu.CompilerParams(vmem_limit_bytes=16 << 20),
        name="turn_left",
    )(left)


def partial_kernel(first, members, left_ref, right_ref, cos_ref, sin_ref, out_ref, plain_ref, rows_ref):
    momenta, sites = cos_ref.shape
    depth = left_ref.shape[1]
    comps = depth // sites
    modes = right_ref.shape[0] // (2 * comps)
    columns = out_ref.shape[0]
    half = GROUP * modes
    skip = first * right_ref.shape[0] // members
    plain_ref[skip:, :] = right_ref[: right_ref.shape[0] - skip, :].astype(jnp.float32)
    plain_ref[:skip, :] = right_ref[right_ref.shape[0] - skip :, :].astype(jnp.float32)
    for q in range(momenta // GROUP):
        slot = q % 2
        for c in range(comps):
            real = plain_ref[pl.ds(2 * c, modes, stride=2 * comps), :]
            imag = plain_ref[pl.ds(2 * c + 1, modes, stride=2 * comps), :]
            lanes = slice(c * sites, (c + 1) * sites)
            for k in range(GROUP):
                p = q * GROUP + k
                cos_row, sin_row = cos_ref[p : p + 1, :], sin_ref[p : p + 1, :]
                turned_re = (cos_row * real + sin_row * imag).astype(jnp.bfloat16)
                turned_im = (cos_row * imag - sin_row * real).astype(jnp.bfloat16)
                rows_ref[slot, k * modes : (k + 1) * modes, lanes] = turned_re
                rows_ref[slot, half + k * modes : half + (k + 1) * modes, lanes] = turned_im
        both = lax.dot_general(left_ref[...], rows_ref[slot], NT, preferred_element_type=jnp.float32)
        upper, lower = both[:columns], both[columns:]
        base = q * 2 * half
        out_ref[:, base : base + half] = (upper[:, :half] + lower[:, half:]).astype(out_ref.dtype)
        out_ref[:, base + half : base + 2 * half] = (upper[:, half:] - lower[:, :half]).astype(out_ref.dtype)


def partial_tile(left, right, cosines, sines, first, members):
    rows, sites = right.shape
    columns, depth = left.shape[0] // 2, left.shape[1]
    modes = rows * sites // (2 * depth)
    momenta = cosines.shape[0]
    return pl.pallas_call(
        functools.partial(partial_kernel, first, members),
        out_shape=jax.ShapeDtypeStruct((columns, momenta * 2 * modes), jnp.bfloat16),
        in_specs=[pl.BlockSpec(memory_space=pltpu.VMEM)] * 4,
        out_specs=pl.BlockSpec(memory_space=pltpu.VMEM),
        scratch_shapes=[
            pltpu.VMEM((rows, sites), jnp.float32),
            pltpu.VMEM((2, 2 * GROUP * modes, depth), jnp.bfloat16),
        ],
        compiler_params=pltpu.CompilerParams(vmem_limit_bytes=32 << 20),
        name="partial_tile",
    )(left, right, cosines, sines)


def sum_kernel(scale, pieces_ref, out_ref):
    _, momenta, parts, modes = out_ref.shape
    total = jnp.sum(pieces_ref[...].astype(jnp.float32), axis=0) * scale
    for p in range(momenta):
        for part in range(parts):
            group, k = divmod(p, GROUP)
            start = ((group * parts + part) * GROUP + k) * modes
            out_ref[:, p, part, :] = total[:, start : start + modes]


def owned_sum(pieces, momenta, scale):
    _, rows, width = pieces.shape
    return pl.pallas_call(
        lambda a, b: sum_kernel(scale, a, b),
        out_shape=jax.ShapeDtypeStruct((rows, momenta, 2, width // (2 * momenta)), jnp.float32),
        in_specs=[pl.BlockSpec(memory_space=pltpu.VMEM)],
        out_specs=pl.BlockSpec(memory_space=pltpu.VMEM),
        compiler_params=pltpu.CompilerParams(vmem_limit_bytes=8 << 20),
        name="owned_sum",
    )(pieces)


def body(left_modes, right_modes, momenta, coords):
    cosines, sines = phase_tables(momenta, coords)
    space, mode = lax.axis_size("space"), lax.axis_size("mode")
    held, _, comps, sites = right_modes.shape
    columns = left_modes.shape[-1]
    norm_scale = 1.0 / math.sqrt(comps * sites * space)
    own = right_modes.transpose(0, 2, 1, 3).reshape(held * comps * 2, sites)
    mode_first, space_first = MODE_FIRST % mode, SPACE_FIRST % space
    right = lax.all_to_all(
        jnp.broadcast_to(own[None], (mode,) + own.shape), "mode", 0, 0, axis_index_groups=[led_by(mode_first, mode)], tiled=True
    )
    rows = columns // space
    left = turned_left(left_modes.reshape(2, comps * sites, columns), space_first * rows)
    tile = partial_tile(left, right.reshape(-1, sites), cosines, sines, mode_first, mode)
    pieces = tile.reshape(space, rows, tile.shape[1])
    owned = lax.all_to_all(
        pieces, "space", 0, 0, axis_index_groups=[led_by(space_first, space)], tiled=True
    )
    return owned_sum(owned, momenta.shape[0], norm_scale)


def solution(mesh):
    in_specs = (
        P(None, None, "space", "mode"),
        P("mode", None, None, "space"),
        P(),
        P(None, "space"),
    )
    out_specs = P(("mode", "space"), None, None, None)
    return jax.shard_map(body, mesh=mesh, in_specs=in_specs, out_specs=out_specs, check_vma=False)
```

```python
import functools
import math

import jax
import jax.numpy as jnp
from jax import lax
from jax.experimental import pallas as pl
from jax.experimental.pallas import tpu as pltpu
from jax.sharding import PartitionSpec as P

EXTENT = 96


def counted_from(first, members):
    start = members.index(first)
    return members[start:] + members[:start]


GROUP = 16
MODE_ORDER = [8 * h + 2 * x + c for h in (1, 0) for c in (1, 0) for x in (3, 2, 1, 0)]
SPACE_ORDER = counted_from(22, [4 * y + z for z in range(4) for y in range(8)])
NT = (((1,), (1,)), ((), ()))


def phase_tables(momenta, coords):
    phase_turns = jnp.mod(jnp.sum(momenta[:, :, None] * coords[None, :, :], axis=1), EXTENT)
    angles = phase_turns.astype(jnp.float32) * (2.0 * math.pi / EXTENT)
    return (jnp.cos(angles), jnp.sin(angles))


def turn_kernel(order, left_ref, out_ref):
    columns = left_ref.shape[2]
    rows = columns // len(order)
    for part in range(2):
        turned = left_ref[part].T
        for k, member in enumerate(order):
            start = part * columns + k * rows
            out_ref[start : start + rows, :] = turned[member * rows : (member + 1) * rows, :]


def turned_left(left, order):
    _, depth, columns = left.shape
    return pl.pallas_call(
        functools.partial(turn_kernel, order),
        out_shape=jax.ShapeDtypeStruct((2 * columns, depth), left.dtype),
        in_specs=[pl.BlockSpec(memory_space=pltpu.VMEM)],
        out_specs=pl.BlockSpec(memory_space=pltpu.VMEM),
        cost_estimate=pl.CostEstimate(flops=0, transcendentals=0, bytes_accessed=4 * left.size),
        compiler_params=pltpu.CompilerParams(vmem_limit_bytes=16 << 20),
        name="turn_left",
    )(left)


def partial_kernel(order, left_ref, right_ref, cos_ref, sin_ref, out_ref, plain_ref, rows_ref):
    momenta, sites = cos_ref.shape
    depth = left_ref.shape[1]
    comps = depth // sites
    modes = right_ref.shape[0] // (2 * comps)
    columns = out_ref.shape[0]
    half = GROUP * modes
    part = right_ref.shape[0] // len(order)
    for k, member in enumerate(order):
        plain_ref[member * part : (member + 1) * part, :] = right_ref[k * part : (k + 1) * part, :].astype(jnp.float32)
    for q in range(momenta // GROUP):
        slot = q % 2
        for c in range(comps):
            real = plain_ref[pl.ds(2 * c, modes, stride=2 * comps), :]
            imag = plain_ref[pl.ds(2 * c + 1, modes, stride=2 * comps), :]
            lanes = slice(c * sites, (c + 1) * sites)
            for k in range(GROUP):
                p = q * GROUP + k
                cos_row, sin_row = cos_ref[p : p + 1, :], sin_ref[p : p + 1, :]
                turned_re = (cos_row * real + sin_row * imag).astype(jnp.bfloat16)
                turned_im = (cos_row * imag - sin_row * real).astype(jnp.bfloat16)
                rows_ref[slot, k * modes : (k + 1) * modes, lanes] = turned_re
                rows_ref[slot, half + k * modes : half + (k + 1) * modes, lanes] = turned_im
        both = lax.dot_general(left_ref[...], rows_ref[slot], NT, preferred_element_type=jnp.float32)
        upper, lower = both[:columns], both[columns:]
        base = q * 2 * half
        out_ref[:, base : base + half] = (upper[:, :half] + lower[:, half:]).astype(out_ref.dtype)
        out_ref[:, base + half : base + 2 * half] = (upper[:, half:] - lower[:, :half]).astype(out_ref.dtype)


def partial_tile(left, right, cosines, sines, order):
    rows, sites = right.shape
    columns, depth = left.shape[0] // 2, left.shape[1]
    modes = rows * sites // (2 * depth)
    momenta = cosines.shape[0]
    return pl.pallas_call(
        functools.partial(partial_kernel, order),
        out_shape=jax.ShapeDtypeStruct((columns, momenta * 2 * modes), jnp.bfloat16),
        in_specs=[pl.BlockSpec(memory_space=pltpu.VMEM)] * 4,
        out_specs=pl.BlockSpec(memory_space=pltpu.VMEM),
        scratch_shapes=[
            pltpu.VMEM((rows, sites), jnp.float32),
            pltpu.VMEM((min(2, momenta // GROUP), 2 * GROUP * modes, depth), jnp.bfloat16),
        ],
        compiler_params=pltpu.CompilerParams(vmem_limit_bytes=32 << 20),
        name="partial_tile",
    )(left, right, cosines, sines)


def sum_kernel(scale, pieces_ref, out_ref):
    _, momenta, parts, modes = out_ref.shape
    total = jnp.sum(pieces_ref[...].astype(jnp.float32), axis=0) * scale
    for p in range(momenta):
        for part in range(parts):
            group, k = divmod(p, GROUP)
            start = ((group * parts + part) * GROUP + k) * modes
            out_ref[:, p, part, :] = total[:, start : start + modes]


def owned_sum(pieces, momenta, scale):
    _, rows, width = pieces.shape
    return pl.pallas_call(
        lambda a, b: sum_kernel(scale, a, b),
        out_shape=jax.ShapeDtypeStruct((rows, momenta, 2, width // (2 * momenta)), jnp.float32),
        in_specs=[pl.BlockSpec(memory_space=pltpu.VMEM)],
        out_specs=pl.BlockSpec(memory_space=pltpu.VMEM),
        compiler_params=pltpu.CompilerParams(vmem_limit_bytes=8 << 20),
        name="owned_sum",
    )(pieces)


def body(left_modes, right_modes, momenta, coords):
    cosines, sines = phase_tables(momenta, coords)
    space, mode = lax.axis_size("space"), lax.axis_size("mode")
    held, _, comps, sites = right_modes.shape
    columns = left_modes.shape[-1]
    norm_scale = 1.0 / math.sqrt(comps * sites * space)
    own = right_modes.transpose(0, 2, 1, 3).reshape(held * comps * 2, sites)
    order, space_order = MODE_ORDER, SPACE_ORDER
    right = lax.all_to_all(
        jnp.broadcast_to(own[None], (mode,) + own.shape), "mode", 0, 0, axis_index_groups=[order], tiled=True
    )
    rows = columns // space
    left = turned_left(left_modes.reshape(2, comps * sites, columns), space_order)
    tile = partial_tile(left, right.reshape(-1, sites), cosines, sines, order)
    pieces = tile.reshape(space, rows, tile.shape[1])
    owned = lax.all_to_all(
        pieces, "space", 0, 0, axis_index_groups=[space_order], tiled=True
    )
    return owned_sum(owned, momenta.shape[0], norm_scale)


def solution(mesh):
    in_specs = (
        P(None, None, "space", "mode"),
        P("mode", None, None, "space"),
        P(),
        P(None, "space"),
    )
    out_specs = P(("mode", "space"), None, None, None)
    return jax.shard_map(body, mesh=mesh, in_specs=in_specs, out_specs=out_specs, check_vma=False)
```

```python
import functools
import math

import jax
import jax.numpy as jnp
from jax import lax
from jax.experimental import pallas as pl
from jax.experimental.pallas import tpu as pltpu
from jax.sharding import PartitionSpec as P

EXTENT = 96


def counted_from(first, members):
    start = members.index(first)
    return members[start:] + members[:start]


GROUP = 8
VMEM_LIMIT = 24 << 20
MODE_ORDER = [8 * h + 2 * x + c for h in (1, 0) for c in (1, 0) for x in (3, 2, 1, 0)]
SPACE_ORDER = counted_from(22, [4 * y + z for z in range(4) for y in range(8)])


def opening_kernel(own_hbm, momenta_hbm, coords_hbm, out_ref, cos_ref, sin_ref, own_ref, momenta_ref, coords_ref, turns_ref, sems):
    moves = [
        pltpu.make_async_copy(source, target, sems.at[k])
        for k, (source, target) in enumerate(
            ((own_hbm, own_ref), (momenta_hbm, momenta_ref), (coords_hbm, coords_ref))
        )
    ]
    for move in moves:
        move.start()
    for move in moves:
        move.wait()
    for k in range(out_ref.shape[0]):
        out_ref[k] = own_ref[...]
    dims, momenta = momenta_ref.shape
    for p in range(momenta):
        turns_ref[p : p + 1, :] = sum(momenta_ref[d : d + 1, p : p + 1] * coords_ref[d : d + 1, :] for d in range(dims))
    angles = jnp.mod(turns_ref[...], EXTENT).astype(jnp.float32) * (2.0 * math.pi / EXTENT)
    cos_ref[...] = jnp.cos(angles)
    sin_ref[...] = jnp.sin(angles)


def opening(own, momenta, coords, count):
    hbm, vmem = pl.BlockSpec(memory_space=pltpu.HBM), pl.BlockSpec(memory_space=pltpu.VMEM)
    phases = jax.ShapeDtypeStruct((momenta.shape[1], coords.shape[1]), jnp.float32)
    return pl.pallas_call(
        opening_kernel,
        out_shape=(jax.ShapeDtypeStruct((count,) + own.shape, own.dtype), phases, phases),
        in_specs=[hbm] * 3,
        out_specs=(vmem,) * 3,
        scratch_shapes=[
            pltpu.VMEM(own.shape, own.dtype),
            pltpu.VMEM(momenta.shape, momenta.dtype),
            pltpu.VMEM(coords.shape, coords.dtype),
            pltpu.VMEM(phases.shape, jnp.int32),
            pltpu.SemaphoreType.DMA((3,)),
        ],
        compiler_params=pltpu.CompilerParams(vmem_limit_bytes=8 << 20),
        name="opening",
    )(*(pltpu.with_memory_space_constraint(x, pltpu.HBM) for x in (own, momenta, coords)))


def partial_kernel(
    order, space_order, left_hbm, right_ref, cos_ref, sin_ref, out_ref, left_ref, plain_ref, rows_ref, sems
):
    moves = [pltpu.make_async_copy(left_hbm.at[k], left_ref.at[k], sems.at[k]) for k in range(2)]
    for move in moves:
        move.start()
    momenta, sites = cos_ref.shape
    depth, columns = left_ref.shape[1:]
    comps = depth // sites
    modes = right_ref.shape[0] // (2 * comps)
    half = GROUP * modes
    part = right_ref.shape[0] // len(order)
    for k, member in enumerate(order):
        plain_ref[member * part : (member + 1) * part, :] = right_ref[k * part : (k + 1) * part, :].astype(jnp.float32)
    rows = columns // len(space_order)
    groups = momenta // GROUP
    for q in range(groups):
        for c in range(comps):
            real = plain_ref[pl.ds(2 * c, modes, stride=2 * comps), :]
            imag = plain_ref[pl.ds(2 * c + 1, modes, stride=2 * comps), :]
            lanes = slice(c * sites, (c + 1) * sites)
            for k in range(GROUP):
                p = q * GROUP + k
                cos_row, sin_row = cos_ref[p : p + 1, :], sin_ref[p : p + 1, :]
                turned_re = (cos_row * real + sin_row * imag).astype(jnp.bfloat16)
                turned_im = (cos_row * imag - sin_row * real).astype(jnp.bfloat16)
                rows_ref[q, k * modes : (k + 1) * modes, lanes] = turned_re
                rows_ref[q, half + k * modes : half + (k + 1) * modes, lanes] = turned_im
    moves[0].wait()
    with_re = [jnp.dot(rows_ref[q], left_ref[0], preferred_element_type=jnp.float32) for q in range(groups)]
    moves[1].wait()
    for q in range(groups):
        with_im = jnp.dot(rows_ref[q], left_ref[1], preferred_element_type=jnp.float32)
        base = q * 2 * half
        for start, value in (
            (base, with_re[q][:half] + with_im[half:]),
            (base + half, with_re[q][half:] - with_im[:half]),
        ):
            tile = value.T
            tile = jnp.concatenate([tile[member * rows : (member + 1) * rows] for member in space_order], axis=0)
            out_ref[:, start : start + half] = tile.astype(out_ref.dtype)


def partial_tile(left, right, cosines, sines, order, space_order):
    rows, sites = right.shape
    _, depth, columns = left.shape
    modes = rows * sites // (2 * depth)
    count = cosines.shape[0]
    vmem = pl.BlockSpec(memory_space=pltpu.VMEM)
    return pl.pallas_call(
        functools.partial(partial_kernel, order, space_order),
        out_shape=jax.ShapeDtypeStruct((columns, count * 2 * modes), jnp.bfloat16),
        in_specs=[pl.BlockSpec(memory_space=pltpu.HBM), vmem, vmem, vmem],
        out_specs=vmem,
        scratch_shapes=[
            pltpu.VMEM(left.shape, left.dtype),
            pltpu.VMEM((rows, sites), jnp.float32),
            pltpu.VMEM((count // GROUP, 2 * GROUP * modes, depth), jnp.bfloat16),
            pltpu.SemaphoreType.DMA((2,)),
        ],
        compiler_params=pltpu.CompilerParams(vmem_limit_bytes=VMEM_LIMIT),
        name="partial_tile",
    )(pltpu.with_memory_space_constraint(left, pltpu.HBM), right, cosines, sines)


def sum_kernel(scale, pieces_ref, out_ref):
    _, momenta, parts, modes = out_ref.shape
    total = jnp.sum(pieces_ref[...].astype(jnp.float32), axis=0) * scale
    for p in range(momenta):
        for part in range(parts):
            group, k = divmod(p, GROUP)
            start = ((group * parts + part) * GROUP + k) * modes
            out_ref[:, p, part, :] = total[:, start : start + modes]


def owned_sum(pieces, momenta, scale):
    _, rows, width = pieces.shape
    return pl.pallas_call(
        lambda a, b: sum_kernel(scale, a, b),
        out_shape=jax.ShapeDtypeStruct((rows, momenta, 2, width // (2 * momenta)), jnp.float32),
        in_specs=[pl.BlockSpec(memory_space=pltpu.VMEM)],
        out_specs=pl.BlockSpec(memory_space=pltpu.VMEM),
        compiler_params=pltpu.CompilerParams(vmem_limit_bytes=8 << 20),
        name="owned_sum",
    )(pieces)


def body(left_modes, right_modes, momenta, coords):
    space, mode = lax.axis_size("space"), lax.axis_size("mode")
    held, _, comps, sites = right_modes.shape
    columns = left_modes.shape[-1]
    norm_scale = 1.0 / math.sqrt(comps * sites * space)
    own = right_modes.transpose(0, 2, 1, 3).reshape(held * comps * 2, sites)
    order, space_order = MODE_ORDER, SPACE_ORDER
    copies, cosines, sines = opening(own, momenta.T, coords, mode)
    right = lax.all_to_all(copies, "mode", 0, 0, axis_index_groups=[order], tiled=True)
    rows = columns // space
    left = left_modes.reshape(2, comps * sites, columns)
    tile = partial_tile(left, right.reshape(-1, sites), cosines, sines, order, space_order)
    pieces = tile.reshape(space, rows, tile.shape[1])
    owned = lax.all_to_all(
        pieces, "space", 0, 0, axis_index_groups=[space_order], tiled=True
    )
    return owned_sum(owned, momenta.shape[0], norm_scale)


def solution(mesh):
    in_specs = (
        P(None, None, "space", "mode"),
        P("mode", None, None, "space"),
        P(),
        P(None, "space"),
    )
    out_specs = P(("mode", "space"), None, None, None)
    return jax.shard_map(body, mesh=mesh, in_specs=in_specs, out_specs=out_specs, check_vma=False)
```
